256 devices in a mesh: row: 32 (over z, y_hi, core), col: 8 (over y_lo, x).
Axes of the slice: x: 4, y: 4 (y_hi: 2, y_lo: 2; y = y_hi * 2 + y_lo), z: 8, core: 2. Of those that a mesh axis runs over, the one named last changes fastest.
Arguments:
- p_vals: float32 [128, 16, 128, 128], P('row', 'col'), may hold values from -2 to 2
- p_cols: int32 [128, 16], P('row'), may hold values from 0 to 127, as said below
- out_cols: int32 [128, 16], P('row'), may hold values from 0 to 127, as said below
Outputs:
- c_vals: float32 [128, 16, 128, 128], P('row', 'col')
The draws below stay inside these ranges and needn't reach their ends.
Inputs may be any that keep to these rules, and one draw needn't show every extreme that they name: Block column indices; p_cols[i, s] // 4 equals (i // 4 + s // 2 - t) mod 32 for some t of 0, 1, 2, 3. `out_cols`: each output block column is p_cols[p_cols[i, s], s2] for some slots s and s2.
All inputs are finite; a program needn't handle non-finite values.
Results may differ from the reference program's by a relative error of at most 0.0003.
Values sent between devices are 32-bit elements; how exact they have to be, the bound alone decides.
A program may use at most 64 MiB of HBM per device.

```python
import jax
import jax.numpy as jnp
from jax import lax

BS = 128
BR = 4
S_DEV = 2
NB = 128
S = 16
SO = 16
N_ROW = 32


def pattern_both(key):
    key_pat = jax.random.fold_in(key, 11)
    k_off, k_loc, k_s, k_t = jax.random.split(key_pat, 4)
    group = jnp.arange(NB, dtype=jnp.int32) // BR
    slot_dev = jnp.arange(S, dtype=jnp.int32) // S_DEV
    step_off = jax.random.randint(k_off, (NB, S), 0, 4, dtype=jnp.int32)
    local_row = jax.random.randint(k_loc, (NB, S), 0, BR, dtype=jnp.int32)
    target = (group[:, None] + slot_dev[None, :] - step_off) % N_ROW
    cols = target * BR + local_row
    first = jax.random.randint(k_s, (NB, SO), 0, S, dtype=jnp.int32)
    second = jax.random.randint(k_t, (NB, SO), 0, S, dtype=jnp.int32)
    middle = jnp.take_along_axis(cols, first, axis=1)
    outs = cols[middle, second]
    return (cols, outs)


def draw_p_cols(key, part):
    return pattern_both(key)[0]


def draw_out_cols(key, part):
    return pattern_both(key)[1]


def levels(stream_key, dims, pieces, smallest, largest):
    level, own = 1.0, jax.random.fold_in(stream_key, 6)
    for position, parts in pieces:
        draws = jnp.exp(jax.random.uniform(jax.random.fold_in(own, position), (parts,), jnp.float32, smallest / len(pieces), largest / len(pieces)))
        level = level * jnp.repeat(draws, dims[position] // parts).reshape([-1 if axis == position else 1 for axis in range(len(dims))])
    return level


def normal_values(own_key, extent, scale, reach, pieces=(), kind=jnp.bfloat16):
    array = scale * jax.random.normal(own_key, extent, jnp.float32)
    if pieces:
        array = array * levels(own_key, extent, pieces, -0.22, 0.18)
    return jnp.clip(array, -reach, reach).astype(kind)


def setup_inputs(seed: int = 0) -> dict:
    key_list = jax.random.split(jax.random.key(seed), 4)
    p_vals = normal_values(key_list[0], (NB, S, BS, BS), 0.3, 2.0, ((0, 32), (1, 8)), jnp.float32)
    p_cols = draw_p_cols(jax.random.fold_in(key_list[3], 71), 0)
    out_cols = draw_out_cols(jax.random.fold_in(key_list[3], 71), 0)
    return {"p_vals": p_vals, "p_cols": p_cols, "out_cols": out_cols}


def reference(p_vals, p_cols, out_cols):
    group = jnp.arange(NB, dtype=jnp.int32) // BR
    slot_dev = jnp.arange(S, dtype=jnp.int32) // S_DEV
    offset = (group[:, None] + slot_dev[None, :] - p_cols // BR) % N_ROW
    window = (offset < 3).astype(jnp.float32)

    def one_row(items):
        vals_row, cols_row, outs_row, weight_row = items
        blocks = p_vals[cols_row]
        inner = p_cols[cols_row]
        match = (inner[:, :, None] == outs_row[None, None, :]).astype(jnp.float32)
        mixed = jnp.einsum("sto,stab->soab", match, blocks, precision=lax.Precision.HIGHEST)
        left = vals_row * weight_row[:, None, None]
        return jnp.einsum("sab,sobc->oac", left, mixed, precision=lax.Precision.HIGHEST)

    return lax.map(one_row, (p_vals, p_cols, out_cols, window))
```

```python
import jax
import jax.numpy as jnp
from jax import lax
from jax.experimental import pallas as pl
from jax.experimental.pallas import tpu as pltpu
from jax.sharding import PartitionSpec as P

MESH = pl.DeviceIdType.MESH
F32 = jnp.float32
BF16 = jnp.bfloat16
NX, NY, NZ = 4, 4, 8


def up(v, d, n):
    return lax.rem(v + (d + n), n)


def kernel(meta_ref, p_ref, out_ref, pt, tb, mbuf, sm, ag, bg, rot, stage, pvs, mt, aw, ct, r1, r2, fo, fi,
           tbs, tbr, ms, mr, ays, ayr, axs, axr, zs, zr, cs, cr, ys, yr, fs, fr, loc):
    row = lax.axis_index("row")
    col = lax.axis_index("col")
    z, yh, q = row // 4, lax.rem(row // 2, 2), lax.rem(row, 2)
    yl, x = col // 4, lax.rem(col, 4)
    y = 2 * yh + yl

    def dev(x_, y_, z_, q_):
        return (z_ * 4 + (y_ // 2) * 2 + q_, lax.rem(y_, 2) * 4 + x_)

    def rcopy(src, dst, s, r, to):
        return pltpu.make_async_remote_copy(
            src_ref=src, dst_ref=dst, send_sem=s, recv_sem=r, device_id=to, device_id_type=MESH
        )

    plane = [(dx, dy) for dy in range(NY) for dx in range(NX) if (dx, dy) != (0, 0)]
    metas = [(lev, dh, dq) for lev in range(4) for dh in range(2) for dq in range(2) if (lev, dh, dq) != (1, 0, 0)]

    def flip(v, d):
        return lax.rem(v + d, 2)

    def level_dev(dz, dh, dq):
        return dev(x, 2 * flip(yh, dh) + yl, up(z, dz, NZ), flip(q, dq))

    barrier = pltpu.get_barrier_semaphore()
    for dx, dy in plane:
        pl.semaphore_signal(barrier, inc=1, device_id=dev(up(x, -dx, NX), up(y, -dy, NY), z, q), device_id_type=MESH)
    for lev, dh, dq in metas:
        pl.semaphore_signal(barrier, inc=1, device_id=level_dev(lev - 1, dh, dq), device_id_type=MESH)

    lane = lax.broadcasted_iota(jnp.int32, (128, 128), 1) // 32
    for e in range(2):
        for l in range(4):
            pt[l, e] = p_ref[l, e].T
        for yy in range(NY):
            packed = None
            for l in range(4):
                t = pt[l, e]
                if l != yy:
                    t = pltpu.roll(t, (32 * (l - yy)) % 128, 1)
                packed = t if packed is None else jnp.where(lane == l, t, packed)
            for xx in range(NX):
                tb[yy, xx, e] = packed[32 * xx:32 * xx + 32].reshape(4, 8, 128)

    pl.semaphore_wait(barrier, len(plane) + len(metas))

    own = [pltpu.make_async_copy(tb.at[y, x], bg.at[q, 1, yh, pl.ds(2 * col, 2)], loc.at[0]),
           pltpu.make_async_copy(meta_ref, mbuf.at[q * 8 + 2 + yh], loc.at[1]),
           pltpu.make_async_copy(pt.at[:, :, pl.ds(32 * y, 32)], ag.at[x, y], loc.at[2])]
    for c in own:
        c.start()
    sends = []
    for n, (dx, dy) in enumerate(plane):
        xx, yy = up(x, dx, NX), up(y, dy, NY)
        c = rcopy(tb.at[yy, xx], bg.at[q, 1, yh, pl.ds(2 * col, 2)], tbs.at[n], tbr.at[n], dev(xx, yy, z, q))
        c.start()
        sends.append(c)
    msends = []
    for n, (lev, dh, dq) in enumerate(metas):
        c = rcopy(meta_ref, mbuf.at[q * 8 + lev * 2 + yh], ms.at[n], mr.at[n], level_dev(1 - lev, dh, dq))
        c.start()
        msends.append(c)
    asends = []
    for dy in range(1, NY):
        yy = up(y, dy, NY)
        c = rcopy(pt.at[:, :, pl.ds(32 * yy, 32)], ag.at[x, y], ays.at[dy], ayr.at[dy], dev(x, yy, z, q))
        c.start()
        asends.append(c)
    for c in own:
        c.wait()
    for c in sends:
        c.wait_recv()

    zdn, zup = up(z, -1, NZ), up(z, 1, NZ)
    lower, upper, mate = dev(x, y, zdn, q), dev(x, y, zup, q), dev(x, y, z, 1 - q)
    z2 = rcopy(bg.at[q, 1], bg.at[q, 2], zs.at[0], zr.at[0], lower)
    z0 = rcopy(bg.at[q, 1, 1], bg.at[q, 0, 1], zs.at[1], zr.at[1], upper)
    c1 = rcopy(bg.at[q, 1], bg.at[q, 1], cs.at[0], cr.at[0], mate)
    z2.start()
    z0.start()
    c1.start()

    for c in asends:
        c.wait_recv()
    xp, xm, xf = up(x, 1, NX), up(x, -1, NX), up(x, 2, NX)
    right, left = dev(xp, y, z, q), dev(xm, y, z, q)
    x0 = rcopy(ag.at[x], ag.at[x], axs.at[0], axr.at[0], right)
    x1 = rcopy(ag.at[x], ag.at[x], axs.at[1], axr.at[1], left)
    x0.start()
    x1.start()

    for c in msends:
        c.wait()
    mc = pltpu.make_async_copy(mbuf, sm, loc.at[3])
    mc.start()

    def expand(qs, lev, h):
        def step(s, carry):
            t = bg[qs, lev, h, s].reshape(32, 128)
            for k in range(4):
                u = t if k == 0 else pltpu.roll(t, 32 * k, 1)
                rot[k, qs * 8 + lev * 2 + h, s] = u.reshape(4, 8, 128)
            return carry
        lax.fori_loop(0, 16, step, 0)

    expand(q, 1, 0)
    expand(q, 1, 1)

    z2.wait_recv()
    z3a = rcopy(bg.at[q, 2, 0], bg.at[q, 3, 0], zs.at[2], zr.at[2], lower)
    z3b = rcopy(bg.at[q, 2, 1], bg.at[q, 3, 1], zs.at[3], zr.at[3], lower)
    z3a.start()

    @pl.when(q == 0)
    def _():
        z3b.start()

    c2 = rcopy(bg.at[q, 2], bg.at[q, 2], cs.at[1], cr.at[1], mate)
    c2.start()
    z0.wait_recv()
    c0 = rcopy(bg.at[1, 0, 1], bg.at[1, 0, 1], cs.at[4], cr.at[4], mate)

    @pl.when(q == 1)
    def _():
        c0.start()

    c1.wait_recv()
    expand(1 - q, 1, 0)
    expand(1 - q, 1, 1)

    x0.wait_recv()
    x1.wait_recv()
    x2 = rcopy(ag.at[xm, pl.ds(0, 2)], ag.at[xm, pl.ds(0, 2)], axs.at[2], axr.at[2], right)
    x3 = rcopy(ag.at[xp, pl.ds(2, 2)], ag.at[xp, pl.ds(2, 2)], axs.at[3], axr.at[3], left)
    x2.start()
    x3.start()

    expand(q, 2, 0)
    expand(q, 2, 1)
    expand(q, 0, 1)

    @pl.when(q == 0)
    def _():
        c0.wait_recv()
        expand(1, 0, 1)

    c2.wait_recv()
    expand(1 - q, 2, 0)
    expand(1 - q, 2, 1)
    z3a.wait_recv()
    c3a = rcopy(bg.at[q, 3, 0], bg.at[q, 3, 0], cs.at[2], cr.at[2], mate)
    c3b = rcopy(bg.at[0, 3, 1], bg.at[0, 3, 1], cs.at[3], cr.at[3], mate)
    c3a.start()
    expand(q, 3, 0)

    @pl.when(q == 0)
    def _():
        z3b.wait_recv()
        c3b.start()
        expand(0, 3, 1)

    c3a.wait_recv()
    expand(1 - q, 3, 0)

    @pl.when(q == 1)
    def _():
        c3b.wait_recv()
        expand(0, 3, 1)

    x2.wait_recv()
    x3.wait_recv()
    mc.wait()

    lane8 = lax.broadcasted_iota(jnp.int32, (8, 128), 1) // 32
    sel = [lane8 == j for j in range(3)]

    def spread(v):
        r = jnp.where(sel[2], v[2], v[3])
        r = jnp.where(sel[1], v[1], r)
        return jnp.where(sel[0], v[0], r)

    def product(h, l, s4):
        mine = q * 8 + 2 + h
        slot, kl, rt, win = [], [], [], []
        for j in range(4):
            s = 4 * s4 + j
            k = sm[mine, l, s]
            g = k // 4
            kk = lax.rem(k, 4)
            off = lax.rem(row // 4 * 4 + 2 * h + q + s // 2 - g + 64, 32)
            w = off < 3
            lev = jnp.where(w, lax.rem(g // 4 - z + 9, 8), 1)
            slot.append(lax.rem(g, 2) * 8 + lev * 2 + lax.rem(g // 2, 2))
            kl.append(kk)
            rt.append(lax.rem(j + 4 - kk, 4))
            win.append(w)
        for s2 in range(16):
            stage[s2] = spread([rot[rt[j], slot[j], s2] for j in range(4)])
            pvs[s2] = spread([jnp.where(win[j], sm[slot[j], kl[j], s2], -1) for j in range(4)])

        def some(oq, carry):
            oc = [sm[mine, l, 16 + oq * 4 + n] for n in range(4)]
            acc = [jnp.zeros((4, 8, 128), F32)] * 4
            for s2 in range(16):
                b = stage[s2]
                v = pvs[s2]
                for n in range(4):
                    acc[n] = acc[n] + jnp.where((v == oc[n])[None], b, 0.0)
            for n in range(4):
                a = acc[n].reshape(32, 128)
                hi = a.astype(BF16)
                lo = (a - hi.astype(F32)).astype(BF16)
                at = pl.ds(pl.multiple_of(oq * 128 + n * 32, 32), 32)
                mt[at, 0:128] = hi
                mt[at, 128:256] = lo
            return carry

        lax.fori_loop(0, 4, some, 0)
        a = ag[pl.ds(2 * (s4 % 2), 2), 2 * h + s4 // 2, l].reshape(128, 128)
        hi = a.astype(BF16)
        aw[0:128, 0:128] = hi
        aw[0:128, 128:256] = (a - hi.astype(F32)).astype(BF16)
        aw[128:256, 0:128] = hi
        r = jnp.dot(mt[...], aw[...], preferred_element_type=F32)
        r = r[:, :128] + r[:, 128:]
        for half in range(2):
            part = r[256 * half:256 * half + 256]
            if s4 == 0:
                ct[h, half, l] = part
            else:
                ct[h, half, l] = ct[h, half, l] + part

    aw[128:256, 128:256] = jnp.zeros((128, 128), BF16)
    for s4 in range(4):
        def step(i, carry, s4=s4):
            product(i // 4, lax.rem(i, 4), s4)
            return carry
        lax.fori_loop(0, 8, step, 0)

    yp, ym, yf = up(y, 1, NY), up(y, -1, NY), up(y, 2, NY)
    above, below = dev(x, yp, z, q), dev(x, ym, z, q)

    def piece(y_):
        return ct.at[y_ // 2, lax.rem(y_, 2)]

    s1a = rcopy(piece(yf).at[pl.ds(0, 2)], r1.at[0], ys.at[0], yr.at[0], above)
    s1b = rcopy(piece(yf).at[pl.ds(2, 2)], r1.at[1], ys.at[1], yr.at[1], below)
    s1a.start()
    s1b.start()
    s1a.wait_recv()
    a = piece(yp).at[pl.ds(0, 2)]
    a[...] = a[...] + r1[0]
    s2a = rcopy(piece(yp), r2.at[0], ys.at[2], yr.at[2], above)
    s2a.start()
    s1b.wait_recv()
    b = piece(ym).at[pl.ds(2, 2)]
    b[...] = b[...] + r1[1]
    s2b = rcopy(piece(ym), r2.at[1], ys.at[3], yr.at[3], below)
    s2b.start()
    s2a.wait_recv()
    s2b.wait_recv()
    mine = piece(y)
    for l in range(4):
        t = mine[l] + r2[0, l] + r2[1, l]
        for xx in range(NX):
            fo[xx, l] = t[64 * xx:64 * xx + 64]

    fsends = []
    for dx in range(1, NX):
        xx = up(x, dx, NX)
        c = rcopy(fo.at[xx], fi.at[x], fs.at[dx], fr.at[dx], dev(xx, y, z, q))
        c.start()
        fsends.append(c)
    lf = pltpu.make_async_copy(fo.at[x], fi.at[x], loc.at[4])
    lf.start()
    lf.wait()
    for c in fsends:
        c.wait_recv()
    for l in range(4):
        for e in range(2):
            t = jnp.concatenate([fi[xx, l, 32 * e:32 * e + 32] for xx in range(NX)], axis=0)
            out_ref[l, e] = t.T

    for c in sends + asends + fsends + [z2, z0, c1, c2, z3a, c3a, x0, x1, x2, x3, s1a, s1b, s2a, s2b]:
        c.wait_send()

    @pl.when(q == 0)
    def _():
        z3b.wait_send()
        c3b.wait_send()

    @pl.when(q == 1)
    def _():
        c0.wait_send()


def on_device(p_vals, p_cols, out_cols):
    meta = jnp.pad(jnp.concatenate([p_cols, out_cols], axis=1), ((0, 4), (0, 96)))
    dma = pltpu.SemaphoreType.DMA
    vm = pltpu.VMEM
    return pl.pallas_call(
        kernel,
        out_shape=jax.ShapeDtypeStruct((4, 2, 128, 128), F32),
        in_specs=[pl.BlockSpec(memory_space=pltpu.VMEM)] * 2,
        out_specs=pl.BlockSpec(memory_space=pltpu.VMEM),
        scratch_shapes=[
            vm((4, 2, 128, 128), F32),
            vm((4, 4, 2, 4, 8, 128), F32),
            vm((16, 8, 128), jnp.int32),
            pltpu.SMEM((16, 8, 128), jnp.int32),
            vm((4, 4, 4, 2, 32, 128), F32),
            vm((2, 4, 2, 16, 4, 8, 128), F32),
            vm((4, 16, 16, 4, 8, 128), F32),
            vm((16, 4, 8, 128), F32),
            vm((16, 8, 128), jnp.int32),
            vm((512, 256), BF16),
            vm((256, 256), BF16),
            vm((2, 2, 4, 256, 128), F32),
            vm((2, 2, 256, 128), F32),
            vm((2, 4, 256, 128), F32),
            vm((4, 4, 64, 128), F32),
            vm((4, 4, 64, 128), F32),
            dma((15,)), dma((15,)), dma((15,)), dma((15,)), dma((4,)), dma((4,)), dma((4,)), dma((4,)),
            dma((4,)), dma((4,)), dma((5,)), dma((5,)), dma((4,)), dma((4,)), dma((4,)), dma((4,)), dma((5,)),
        ],
        compiler_params=pltpu.CompilerParams(collective_id=0, has_side_effects=True),
        name="square",
    )(meta, p_vals)


def solution(mesh):
    placed = (P("row", "col", None, None), P("row", None), P("row", None))
    return jax.shard_map(
        on_device,
        mesh=mesh,
        in_specs=placed,
        out_specs=P("row", "col", None, None),
        check_vma=False,
    )
```

```python
import jax
import jax.numpy as jnp
from jax import lax
from jax.experimental import pallas as pl
from jax.experimental.pallas import tpu as pltpu
from jax.sharding import PartitionSpec as P

MESH = pl.DeviceIdType.MESH
F32 = jnp.float32
BF16 = jnp.bfloat16
NX, NY, NZ = 4, 4, 8


def up(v, d, n):
    return lax.rem(v + (d + n), n)


def kernel(meta_ref, p_ref, out_ref, pt, tb, mbuf, sm, ix, ixs, ag, bg, rot, pvs, mt, aw, ct, r1, r2, fo, fi,
           tbs, tbr, ms, mr, ays, ayr, axs, axr, zs, zr, cs, cr, ys, yr, fs, fr, loc):
    row = lax.axis_index("row")
    col = lax.axis_index("col")
    z, yh, q = row // 4, lax.rem(row // 2, 2), lax.rem(row, 2)
    yl, x = col // 4, lax.rem(col, 4)
    y = 2 * yh + yl

    def dev(x_, y_, z_, q_):
        return (z_ * 4 + (y_ // 2) * 2 + q_, lax.rem(y_, 2) * 4 + x_)

    def rcopy(src, dst, s, r, to):
        return pltpu.make_async_remote_copy(
            src_ref=src, dst_ref=dst, send_sem=s, recv_sem=r, device_id=to, device_id_type=MESH
        )

    plane = [(dx, dy) for dy in range(NY) for dx in range(NX) if (dx, dy) != (0, 0)]
    metas = [(lev, dh, dq) for lev in range(4) for dh in range(2) for dq in range(2) if (lev, dh, dq) != (1, 0, 0)]

    def flip(v, d):
        return lax.rem(v + d, 2)

    def level_dev(dz, dh, dq):
        return dev(x, 2 * flip(yh, dh) + yl, up(z, dz, NZ), flip(q, dq))

    barrier = pltpu.get_barrier_semaphore()
    for dx, dy in plane:
        pl.semaphore_signal(barrier, inc=1, device_id=dev(up(x, -dx, NX), up(y, -dy, NY), z, q), device_id_type=MESH)
    for lev, dh, dq in metas:
        pl.semaphore_signal(barrier, inc=1, device_id=level_dev(lev - 1, dh, dq), device_id_type=MESH)

    lane = lax.broadcasted_iota(jnp.int32, (128, 128), 1) // 32
    for e in range(2):
        for l in range(4):
            pt[l, e] = p_ref[l, e].T
        for yy in range(NY):
            packed = None
            for l in range(4):
                t = pt[l, e]
                if l != yy:
                    t = pltpu.roll(t, (32 * (l - yy)) % 128, 1)
                packed = t if packed is None else jnp.where(lane == l, t, packed)
            for xx in range(NX):
                tb[yy, xx, e] = packed[32 * xx:32 * xx + 32].reshape(4, 8, 128)

    pl.semaphore_wait(barrier, len(plane) + len(metas))

    own = [pltpu.make_async_copy(tb.at[y, x], bg.at[q, 1, yh, pl.ds(2 * col, 2)], loc.at[0]),
           pltpu.make_async_copy(meta_ref, mbuf.at[q * 8 + 2 + yh], loc.at[1]),
           pltpu.make_async_copy(pt.at[:, :, pl.ds(32 * y, 32)], ag.at[x, y], loc.at[2])]
    for c in own:
        c.start()
    sends = []
    for n, (dx, dy) in enumerate(plane):
        xx, yy = up(x, dx, NX), up(y, dy, NY)
        c = rcopy(tb.at[yy, xx], bg.at[q, 1, yh, pl.ds(2 * col, 2)], tbs.at[n], tbr.at[n], dev(xx, yy, z, q))
        c.start()
        sends.append(c)
    msends = []
    for n, (lev, dh, dq) in enumerate(metas):
        c = rcopy(meta_ref, mbuf.at[q * 8 + lev * 2 + yh], ms.at[n], mr.at[n], level_dev(1 - lev, dh, dq))
        c.start()
        msends.append(c)
    asends = []
    for dy in range(1, NY):
        yy = up(y, dy, NY)
        c = rcopy(pt.at[:, :, pl.ds(32 * yy, 32)], ag.at[x, y], ays.at[dy], ayr.at[dy], dev(x, yy, z, q))
        c.start()
        asends.append(c)
    for c in own:
        c.wait()
    for c in sends:
        c.wait_recv()

    zdn, zup = up(z, -1, NZ), up(z, 1, NZ)
    lower, upper, mate = dev(x, y, zdn, q), dev(x, y, zup, q), dev(x, y, z, 1 - q)
    z2 = rcopy(bg.at[q, 1], bg.at[q, 2], zs.at[0], zr.at[0], lower)
    z0 = rcopy(bg.at[q, 1, 1], bg.at[q, 0, 1], zs.at[1], zr.at[1], upper)
    c1 = rcopy(bg.at[q, 1], bg.at[q, 1], cs.at[0], cr.at[0], mate)
    z2.start()
    z0.start()
    c1.start()

    for c in asends:
        c.wait_recv()
    xp, xm, xf = up(x, 1, NX), up(x, -1, NX), up(x, 2, NX)
    right, left = dev(xp, y, z, q), dev(xm, y, z, q)
    x0 = rcopy(ag.at[x], ag.at[x], axs.at[0], axr.at[0], right)
    x1 = rcopy(ag.at[x], ag.at[x], axs.at[1], axr.at[1], left)
    x0.start()
    x1.start()

    for c in msends:
        c.wait()
    mc = pltpu.make_async_copy(mbuf, sm, loc.at[3])
    mc.start()

    mc.wait()
    lane8 = lax.broadcasted_iota(jnp.int32, (8, 128), 1) // 32
    sel = [lane8 == j for j in range(3)]

    def spread(v):
        r = jnp.where(sel[2], v[2], v[3])
        r = jnp.where(sel[1], v[1], r)
        return jnp.where(sel[0], v[0], r)

    def expand(qs, lev, h):
        slot = qs * 8 + lev * 2 + h
        for s in range(16):
            pvs[s] = spread([sm[slot, l, s] for l in range(4)])

        def step(i, carry):
            acc = [jnp.zeros((4, 8, 128), F32)] * 2
            v = [pvs[2 * i + e] for e in range(2)]
            for s in range(16):
                b = bg[qs, lev, h, s]
                w = pvs[s]
                for e in range(2):
                    acc[e] = acc[e] + jnp.where((w == v[e])[None], b, 0.0)
            for e in range(2):
                t = acc[e].reshape(32, 128)
                for k in range(4):
                    u = t if k == 0 else pltpu.roll(t, 32 * k, 1)
                    rot[(k * 16 + slot) * 16 + 2 * i + e] = u.reshape(4, 8, 128)
            return carry
        lax.fori_loop(0, 8, step, 0)

    rot[1024] = jnp.zeros((4, 8, 128), F32)

    def pick(i, carry):
        h, l, s4 = i // 16, lax.rem(i // 4, 4), lax.rem(i, 4)
        mine = q * 8 + 2 + h
        outs = mbuf[mine, pl.ds(l, 1)]
        for j in range(4):
            s = 4 * s4 + j
            k = sm[mine, l, s]
            g = k // 4
            kk = lax.rem(k, 4)
            w = lax.rem(row // 4 * 4 + 2 * h + q + s // 2 - g + 64, 32) < 3
            lev = jnp.where(w, lax.rem(g // 4 - z + 9, 8), 1)
            slot = lax.rem(g, 2) * 8 + lev * 2 + lax.rem(g // 2, 2)
            base = (lax.rem(j + 4 - kk, 4) * 16 + slot) * 16
            v = jnp.full((1, 128), 1024, jnp.int32)
            for s2 in reversed(range(16)):
                v = jnp.where(outs == jnp.where(w, sm[slot, kk, s2], -1), base + s2, v)
            ix[pl.ds(i * 4 + j, 1)] = v
        return carry

    lax.fori_loop(0, 32, pick, 0)
    ic = pltpu.make_async_copy(ix, ixs, loc.at[3])
    ic.start()

    expand(q, 1, 0)
    expand(q, 1, 1)

    z2.wait_recv()
    z3a = rcopy(bg.at[q, 2, 0], bg.at[q, 3, 0], zs.at[2], zr.at[2], lower)
    z3b = rcopy(bg.at[q, 2, 1], bg.at[q, 3, 1], zs.at[3], zr.at[3], lower)
    z3a.start()

    @pl.when(q == 0)
    def _():
        z3b.start()

    c2 = rcopy(bg.at[q, 2], bg.at[q, 2], cs.at[1], cr.at[1], mate)
    c2.start()
    z0.wait_recv()
    c0 = rcopy(bg.at[1, 0, 1], bg.at[1, 0, 1], cs.at[4], cr.at[4], mate)

    @pl.when(q == 1)
    def _():
        c0.start()

    c1.wait_recv()
    expand(1 - q, 1, 0)
    expand(1 - q, 1, 1)

    x0.wait_recv()
    x1.wait_recv()
    x2 = rcopy(ag.at[xm, pl.ds(0, 2)], ag.at[xm, pl.ds(0, 2)], axs.at[2], axr.at[2], right)
    x3 = rcopy(ag.at[xp, pl.ds(2, 2)], ag.at[xp, pl.ds(2, 2)], axs.at[3], axr.at[3], left)
    x2.start()
    x3.start()

    expand(q, 2, 0)
    expand(q, 2, 1)
    expand(q, 0, 1)

    @pl.when(q == 0)
    def _():
        c0.wait_recv()
        expand(1, 0, 1)

    c2.wait_recv()
    expand(1 - q, 2, 0)
    expand(1 - q, 2, 1)
    def product(h, l, s4, m):
        for o in range(16):
            a = spread([rot[ixs[(h * 4 + l) * 16 + 4 * s4 + j, 16 + o]] for j in range(4)]).reshape(32, 128)
            hi = a.astype(BF16)
            mt[m, 32 * o:32 * o + 32, 0:128] = hi
            mt[m, 32 * o:32 * o + 32, 128:256] = (a - hi.astype(F32)).astype(BF16)
        a = ag[pl.ds(2 * (s4 % 2), 2), 2 * h + s4 // 2, l].reshape(128, 128)
        hi = a.astype(BF16)
        aw[m, 0:128, 0:128] = hi
        aw[m, 0:128, 128:256] = (a - hi.astype(F32)).astype(BF16)
        aw[m, 128:256, 0:128] = hi
        r = jnp.dot(mt[m], aw[m], preferred_element_type=F32)
        r = r[:, :128] + r[:, 128:]
        for half in range(2):
            part = r[256 * half:256 * half + 256]
            if s4 == 0:
                ct[h, half, l] = part
            else:
                ct[h, half, l] = ct[h, half, l] + part

    for m in range(2):
        aw[m, 128:256, 128:256] = jnp.zeros((128, 128), BF16)

    def products(h, s4):
        def step(i, carry):
            for m in range(2):
                product(h, 2 * i + m, s4, m)
            return carry
        lax.fori_loop(0, 2, step, 0)

    x2.wait_recv()
    x3.wait_recv()
    ic.wait()
    for s4 in range(2):
        products(1 - yh, s4)
        products(yh, s4)

    z3a.wait_recv()
    c3a = rcopy(bg.at[q, 3, 0], bg.at[q, 3, 0], cs.at[2], cr.at[2], mate)
    c3b = rcopy(bg.at[0, 3, 1], bg.at[0, 3, 1], cs.at[3], cr.at[3], mate)
    c3a.start()
    expand(q, 3, 0)

    @pl.when(q == 0)
    def _():
        z3b.wait_recv()
        c3b.start()
        expand(0, 3, 1)

    c3a.wait_recv()
    expand(1 - q, 3, 0)

    @pl.when(q == 1)
    def _():
        c3b.wait_recv()
        expand(0, 3, 1)

    products(1 - yh, 2)
    products(1 - yh, 3)

    yp, ym, yf = up(y, 1, NY), up(y, -1, NY), up(y, 2, NY)
    above, below = dev(x, yp, z, q), dev(x, ym, z, q)

    def piece(y_):
        return ct.at[y_ // 2, lax.rem(y_, 2)]

    s1a = rcopy(piece(yf).at[pl.ds(0, 2)], r1.at[0], ys.at[0], yr.at[0], above)
    s1b = rcopy(piece(yf).at[pl.ds(2, 2)], r1.at[1], ys.at[1], yr.at[1], below)
    s1a.start()
    s1b.start()
    products(yh, 2)
    products(yh, 3)
    s1a.wait_recv()
    a = piece(yp).at[pl.ds(0, 2)]
    a[...] = a[...] + r1[0]
    s2a = rcopy(piece(yp), r2.at[0], ys.at[2], yr.at[2], above)
    s2a.start()
    s1b.wait_recv()
    b = piece(ym).at[pl.ds(2, 2)]
    b[...] = b[...] + r1[1]
    s2b = rcopy(piece(ym), r2.at[1], ys.at[3], yr.at[3], below)
    s2b.start()
    s2a.wait_recv()
    s2b.wait_recv()
    mine = piece(y)
    for l in range(4):
        t = mine[l] + r2[0, l] + r2[1, l]
        for xx in range(NX):
            fo[xx, l] = t[64 * xx:64 * xx + 64]

    fsends = []
    for dx in range(1, NX):
        xx = up(x, dx, NX)
        c = rcopy(fo.at[xx], fi.at[x], fs.at[dx], fr.at[dx], dev(xx, y, z, q))
        c.start()
        fsends.append(c)
    lf = pltpu.make_async_copy(fo.at[x], fi.at[x], loc.at[4])
    lf.start()
    lf.wait()
    for c in fsends:
        c.wait_recv()
    for l in range(4):
        for e in range(2):
            t = jnp.concatenate([fi[xx, l, 32 * e:32 * e + 32] for xx in range(NX)], axis=0)
            out_ref[l, e] = t.T

    for c in sends + asends + fsends + [z2, z0, c1, c2, z3a, c3a, x0, x1, x2, x3, s1a, s1b, s2a, s2b]:
        c.wait_send()

    @pl.when(q == 0)
    def _():
        z3b.wait_send()
        c3b.wait_send()

    @pl.when(q == 1)
    def _():
        c0.wait_send()


def on_device(p_vals, p_cols, out_cols):
    meta = jnp.pad(jnp.concatenate([p_cols, out_cols], axis=1), ((0, 4), (0, 96)))
    dma = pltpu.SemaphoreType.DMA
    vm = pltpu.VMEM
    return pl.pallas_call(
        kernel,
        out_shape=jax.ShapeDtypeStruct((4, 2, 128, 128), F32),
        in_specs=[pl.BlockSpec(memory_space=pltpu.VMEM)] * 2,
        out_specs=pl.BlockSpec(memory_space=pltpu.VMEM),
        scratch_shapes=[
            vm((4, 2, 128, 128), F32),
            vm((4, 4, 2, 4, 8, 128), F32),
            vm((16, 8, 128), jnp.int32),
            pltpu.SMEM((16, 8, 128), jnp.int32),
            vm((128, 128), jnp.int32),
            pltpu.SMEM((128, 128), jnp.int32),
            vm((4, 4, 4, 2, 32, 128), F32),
            vm((2, 4, 2, 16, 4, 8, 128), F32),
            vm((1025, 4, 8, 128), F32),
            vm((16, 8, 128), jnp.int32),
            vm((2, 512, 256), BF16),
            vm((2, 256, 256), BF16),
            vm((2, 2, 4, 256, 128), F32),
            vm((2, 2, 256, 128), F32),
            vm((2, 4, 256, 128), F32),
            vm((4, 4, 64, 128), F32),
            vm((4, 4, 64, 128), F32),
            dma((15,)), dma((15,)), dma((15,)), dma((15,)), dma((4,)), dma((4,)), dma((4,)), dma((4,)),
            dma((4,)), dma((4,)), dma((5,)), dma((5,)), dma((4,)), dma((4,)), dma((4,)), dma((4,)), dma((5,)),
        ],
        compiler_params=pltpu.CompilerParams(collective_id=0, has_side_effects=True),
        name="square",
    )(meta, p_vals)


def solution(mesh):
    placed = (P("row", "col", None, None), P("row", None), P("row", None))
    return jax.shard_map(
        on_device,
        mesh=mesh,
        in_specs=placed,
        out_specs=P("row", "col", None, None),
        check_vma=False,
    )
```

```python
import jax
import jax.numpy as jnp
from jax import lax
from jax.experimental import pallas as pl
from jax.experimental.pallas import tpu as pltpu
from jax.sharding import PartitionSpec as P

MESH = pl.DeviceIdType.MESH
F32 = jnp.float32
BF16 = jnp.bfloat16
NX, NY, NZ = 4, 4, 8


def up(v, d, n):
    return lax.rem(v + (d + n), n)


def kernel(p_ref, pc_ref, oc_ref, out_ref, pt, tb, mown, mbuf, sm, ix, ixs, ag, bg, rot, pvs, mt, aw, ct, r1, r2, fo, fi,
           tbs, tbr, ms, mr, ays, ayr, axs, axr, afs, afr, zs, zr, cs, cr, us, ur, vs, vr, fs, fr, loc):
    row = lax.axis_index("row")
    col = lax.axis_index("col")
    z, yh, q = lax.div(row, 4), lax.rem(lax.div(row, 2), 2), lax.rem(row, 2)
    yl, x = lax.div(col, 4), lax.rem(col, 4)
    y = 2 * yh + yl

    def dev(x_, y_, z_, q_):
        return (z_ * 4 + lax.div(y_, 2) * 2 + q_, lax.rem(y_, 2) * 4 + x_)

    def rcopy(src, dst, s, r, to):
        return pltpu.make_async_remote_copy(
            src_ref=src, dst_ref=dst, send_sem=s, recv_sem=r, device_id=to, device_id_type=MESH
        )

    started = []

    def go(c):
        c.start()
        started.append(c)
        return c

    plane = [(dx, dy) for dy in range(NY) for dx in range(NX) if (dx, dy) != (0, 0)]
    lower, upper, mate = dev(x, y, up(z, -1, NZ), q), dev(x, y, up(z, 1, NZ), q), dev(x, y, z, 1 - q)
    xp, xm = up(x, 1, NX), up(x, -1, NX)
    right, left = dev(xp, y, z, q), dev(xm, y, z, q)
    yp, ym, yf = up(y, 1, NY), up(y, -1, NY), up(y, 2, NY)
    above, below = dev(x, yp, z, q), dev(x, ym, z, q)

    barrier = pltpu.get_barrier_semaphore()
    for to in [dev(up(x, -dx, NX), up(y, -dy, NY), z, q) for dx, dy in plane] + [lower, upper, mate]:
        pl.semaphore_signal(barrier, inc=1, device_id=to, device_id_type=MESH)

    mown[...] = jnp.zeros((8, 128), jnp.int32)
    mown[0:4, 0:16] = pc_ref[...]
    mown[4:8, 0:16] = oc_ref[...]
    lane = lax.div(lax.broadcasted_iota(jnp.int32, (128, 128), 1), 32)
    for e in range(2):
        for l in range(4):
            pt[l, e] = p_ref[l, e].T
        for yy in range(NY):
            packed = None
            for l in range(4):
                t = pt[l, e]
                if l != yy:
                    t = pltpu.roll(t, (32 * (l - yy)) % 128, 1)
                packed = t if packed is None else jnp.where(lane == l, t, packed)
            for xx in range(NX):
                tb[e, yy, xx] = packed[32 * xx:32 * xx + 32].reshape(4, 8, 128)
    rot[1024] = jnp.zeros((4, 8, 128), F32)
    for m in range(2):
        aw[m, 128:256, 128:256] = jnp.zeros((128, 128), BF16)

    pl.semaphore_wait(barrier, len(plane) + 3)

    my = go(rcopy(mown, mbuf.at[q * 8 + 2 + yh], ms.at[0], mr.at[0], dev(x, yf, z, q)))
    own = [pltpu.make_async_copy(mown, mbuf.at[q * 8 + 2 + yh], loc.at[0])]
    own += [pltpu.make_async_copy(tb.at[e, y, x], bg.at[q, 1, yh, e, col], loc.at[1 + e]) for e in range(2)]
    own += [pltpu.make_async_copy(pt.at[:, :, pl.ds(32 * y, 32)], ag.at[x, y], loc.at[3])]
    for c in own:
        c.start()

    def pieces(e):
        out = []
        for n, (dx, dy) in enumerate(plane):
            xx, yy = up(x, dx, NX), up(y, dy, NY)
            out.append(go(rcopy(tb.at[e, yy, xx], bg.at[q, 1, yh, e, col], tbs.at[e, n], tbr.at[e, n], dev(xx, yy, z, q))))
        return out

    b0 = pieces(0)
    rows_y = pt.at[:, :, pl.ds(32 * y, 32)]

    def beside(src, ys):
        return [rcopy(src, ag.at[x, ys], axs.at[n, ys], axr.at[n, ys], (right, left)[n]) for n in range(2)]

    for c in beside(rows_y, y):
        c.start()
    for dy in (1, 3, 2):
        if dy == 2:
            b1 = pieces(1)
        yy = up(y, dy, NY)
        go(rcopy(pt.at[:, :, pl.ds(32 * yy, 32)], ag.at[x, y], ays.at[dy], ayr.at[y], dev(x, yy, z, q)))

    for c in own:
        c.wait()
    my.wait_recv()
    m2 = go(rcopy(mbuf.at[pl.ds(q * 8 + 2, 2)], mbuf.at[pl.ds(q * 8 + 4, 2)], ms.at[1], mr.at[1], lower))
    m0 = go(rcopy(mbuf.at[q * 8 + 3], mbuf.at[q * 8 + 1], ms.at[2], mr.at[2], upper))
    m2.wait_recv()
    m3 = go(rcopy(mbuf.at[pl.ds(q * 8 + 4, 2)], mbuf.at[pl.ds(q * 8 + 6, 2)], ms.at[3], mr.at[3], lower))

    def level1(e):
        a = go(rcopy(bg.at[q, 1, :, e], bg.at[q, 2, :, e], zs.at[0, e], zr.at[0, e], lower))
        b = go(rcopy(bg.at[q, 1, 1, e], bg.at[q, 0, 1, e], zs.at[1, e], zr.at[1, e], upper))
        return a, b

    for c in b0:
        c.wait_recv()
    za0, zb0 = level1(0)
    m0.wait_recv()
    m3.wait_recv()
    mm = go(rcopy(mbuf.at[pl.ds(q * 8 + 1, 7)], mbuf.at[pl.ds(q * 8 + 1, 7)], ms.at[4], mr.at[4], mate))
    mm.wait_recv()
    mc = pltpu.make_async_copy(mbuf, sm, loc.at[0])
    mc.start()
    mc.wait()

    def pick(i, carry):
        h, l, s4 = lax.div(i, 16), lax.rem(lax.div(i, 4), 4), lax.rem(i, 4)
        mine = q * 8 + 2 + h
        outs = mbuf[mine, pl.ds(4 + l, 1)]
        for j in range(4):
            s = 4 * s4 + j
            k = sm[mine, l, s]
            g = lax.div(k, 4)
            kk = lax.rem(k, 4)
            w = lax.rem(4 * z + 2 * h + q + lax.div(s, 2) - g + 64, 32) < 3
            lev = jnp.where(w, lax.rem(lax.div(g, 4) - z + 9, 8), 1)
            slot = lax.rem(g, 2) * 8 + lev * 2 + lax.rem(lax.div(g, 2), 2)
            base = (lax.rem(j + 4 - kk, 4) * 16 + slot) * 16
            v = jnp.full((1, 128), 1024, jnp.int32)
            for p in range(16):
                v = jnp.where(outs == sm[slot, kk, 2 * (p % 8) + p // 8], base + p, v)
            ix[pl.ds(i * 4 + j, 1)] = jnp.where(w, v, 1024)
        return carry

    lax.fori_loop(0, 32, pick, 0)
    ic = pltpu.make_async_copy(ix, ixs, loc.at[0])
    ic.start()

    for c in b1:
        c.wait_recv()
    za1, zb1 = level1(1)
    c1 = go(rcopy(bg.at[q, 1], bg.at[q, 1], cs.at[0], cr.at[0], mate))

    direct = [beside(ag.at[x, ys], ys) for ys in range(NY)]
    for ys in range(NY):
        @pl.when(y != ys)
        def _(ys=ys):
            rcopy(rows_y, ag.at[x, ys], ays.at[0], ayr.at[ys], right).wait_recv()
            for c in direct[ys]:
                c.start()

    def onward(ys):
        n = ys % 2
        direct[ys][n].wait_recv()
        ref = ag.at[(xm, xp)[n], ys]
        return go(rcopy(ref, ref, afs.at[ys], afr.at[ys], (right, left)[n]))

    lane8 = lax.div(lax.broadcasted_iota(jnp.int32, (8, 128), 1), 32)
    sel = [lane8 == j for j in range(3)]

    def spread(v):
        r = jnp.where(sel[2], v[2], v[3])
        r = jnp.where(sel[1], v[1], r)
        return jnp.where(sel[0], v[0], r)

    def expand(qs, lev, h):
        slot = qs * 8 + lev * 2 + h
        for p in range(16):
            pvs[p] = spread([sm[slot, l, 2 * (p % 8) + p // 8] for l in range(4)])

        def step(i, carry):
            acc = [jnp.zeros((4, 8, 128), F32)] * 2
            v = [pvs[2 * i + n] for n in range(2)]
            for p in range(16):
                b = bg[qs, lev, h, p // 8, p % 8]
                w = pvs[p]
                for n in range(2):
                    acc[n] = acc[n] + jnp.where((w == v[n])[None], b, 0.0)
            for n in range(2):
                t = acc[n].reshape(32, 128)
                for k in range(4):
                    u = t if k == 0 else pltpu.roll(t, 32 * k, 1)
                    rot[(k * 16 + slot) * 16 + 2 * i + n] = u.reshape(4, 8, 128)
            return carry
        lax.fori_loop(0, 8, step, 0)

    def both(qs, lev):
        def step(h, carry):
            expand(qs, lev, h)
            return carry
        lax.fori_loop(0, 2, step, 0)

    def level2(e, za):
        za.wait_recv()
        a = go(rcopy(bg.at[q, 2, 0, e], bg.at[q, 3, 0, e], zs.at[2, e], zr.at[2, e], lower))
        return a

    zc0 = level2(0, za0)
    both(q, 1)
    c1.wait_recv()
    both(1 - q, 1)

    far = [onward(0), onward(1)]
    zc1 = level2(1, za1)
    zd = [rcopy(bg.at[0, 2, 1, e], bg.at[0, 3, 1, e], zs.at[3, e], zr.at[3, e], lower) for e in range(2)]

    @pl.when(q == 0)
    def _():
        for c in zd:
            c.start()

    c2 = go(rcopy(bg.at[q, 2], bg.at[q, 2], cs.at[1], cr.at[1], mate))
    zb0.wait_recv()
    zb1.wait_recv()
    c0 = rcopy(bg.at[1, 0, 1], bg.at[1, 0, 1], cs.at[4], cr.at[4], mate)

    @pl.when(q == 1)
    def _():
        c0.start()

    both(q, 2)
    far += [onward(2), onward(3)]
    c2.wait_recv()
    both(1 - q, 2)

    @pl.when(q == 0)
    def _():
        c0.wait_recv()

    expand(1, 0, 1)

    @pl.when(q == 0)
    def _():
        expand(0, 0, 1)

    def product(h, l, s4, m, first):
        for o in range(16):
            a = spread([rot[ixs[(h * 4 + l) * 16 + 4 * s4 + j, o]] for j in range(4)]).reshape(32, 128)
            hi = a.astype(BF16)
            mt[m, 32 * o:32 * o + 32, 0:128] = hi
            mt[m, 32 * o:32 * o + 32, 128:256] = (a - hi.astype(F32)).astype(BF16)
        a = ag[pl.ds(2 * lax.rem(s4, 2), 2), 2 * h + lax.div(s4, 2), l].reshape(128, 128)
        hi = a.astype(BF16)
        aw[m, 0:128, 0:128] = hi
        aw[m, 0:128, 128:256] = (a - hi.astype(F32)).astype(BF16)
        aw[m, 128:256, 0:128] = hi
        r = jnp.dot(mt[m], aw[m], preferred_element_type=F32)
        r = r[:, :128] + r[:, 128:]
        for half in range(2):
            part = r[256 * half:256 * half + 256]
            ct[h, half, l] = part if first else ct[h, half, l] + part

    def early(h):
        for ys in (2 * h, 2 * h + 1):
            direct[ys][1 - ys % 2].wait_recv()
            far[ys].wait_recv()
        for s4 in range(2):
            def step(i, carry, s4=s4):
                for m in range(2):
                    product(h, 2 * i + m, s4, m, s4 == 0)
                return carry
            lax.fori_loop(0, 2, step, 0)

    ic.wait()
    early(0)
    zc0.wait_recv()
    zc1.wait_recv()
    c3a = go(rcopy(bg.at[q, 3, 0], bg.at[q, 3, 0], cs.at[2], cr.at[2], mate))
    c3b = rcopy(bg.at[0, 3, 1], bg.at[0, 3, 1], cs.at[3], cr.at[3], mate)
    expand(q, 3, 0)
    early(1)

    @pl.when(q == 0)
    def _():
        for c in zd:
            c.wait_recv()
        c3b.start()

    c3a.wait_recv()
    expand(1 - q, 3, 0)

    @pl.when(q == 1)
    def _():
        c3b.wait_recv()
        expand(0, 3, 1)

    def piece(y_, lp, part):
        return ct.at[lax.div(y_, 2), lax.rem(y_, 2), pl.ds(2 * lp, 2), pl.ds(128 * part, 128)]

    def rest(h, lp):
        def step(i, carry):
            for m in range(2):
                product(h, 2 * lp + m, 2 + i, m, False)
            return carry
        lax.fori_loop(0, 2, step, 0)

    def hop1(d, lp):
        return go(rcopy(piece(yf, lp, d), r1.at[d, lp], us.at[d, lp], ur.at[d, lp], (above, below)[d]))

    def hop2(d, part, lp):
        return go(rcopy(piece((yp, ym)[d], lp, part), r2.at[d, pl.ds(2 * lp, 2), pl.ds(128 * part, 128)],
                        vs.at[d, part, lp], vr.at[d, part, lp], (above, below)[d]))

    u, v = {}, {}
    for lp in range(2):
        rest(1 - yh, lp)
        for d in range(2):
            u[d, lp] = hop1(d, lp)
    for lp in range(2):
        rest(yh, lp)
        for d in range(2):
            v[d, 1 - d, lp] = hop2(d, 1 - d, lp)
    for lp in range(2):
        for d in range(2):
            u[d, lp].wait_recv()
            a = piece((yp, ym)[d], lp, d)
            a[...] = a[...] + r1[d, lp]
            v[d, d, lp] = hop2(d, d, lp)

    fsend = {}
    for lp in range(2):
        for d in range(2):
            for part in range(2):
                v[d, part, lp].wait_recv()
        for k in range(2):
            l = 2 * lp + k
            t = ct[yh, yl, l] + r2[0, l] + r2[1, l]
            for xx in range(NX):
                fo[lp, xx, k] = t[64 * xx:64 * xx + 64]
        for dx in range(1, NX):
            xx = up(x, dx, NX)
            fsend[lp, dx] = go(rcopy(fo.at[lp, xx], fi.at[lp, x], fs.at[lp, dx], fr.at[lp, dx], dev(xx, y, z, q)))
        fsend[lp, 0] = pltpu.make_async_copy(fo.at[lp, x], fi.at[lp, x], loc.at[lp])
        fsend[lp, 0].start()
    for lp in range(2):
        fsend[lp, 0].wait()
        for dx in range(1, NX):
            fsend[lp, dx].wait_recv()
        for k in range(2):
            for e in range(2):
                t = jnp.concatenate([fi[lp, xx, k, 32 * e:32 * e + 32] for xx in range(NX)], axis=0)
                out_ref[2 * lp + k, e] = t.T

    for c in started + [c for k in direct for c in k]:
        c.wait_send()

    @pl.when(q == 0)
    def _():
        for c in zd:
            c.wait_send()
        c3b.wait_send()

    @pl.when(q == 1)
    def _():
        c0.wait_send()


def on_device(p_vals, p_cols, out_cols):
    dma = pltpu.SemaphoreType.DMA
    vm = pltpu.VMEM
    return pl.pallas_call(
        kernel,
        out_shape=jax.ShapeDtypeStruct((4, 2, 128, 128), F32),
        in_specs=[pl.BlockSpec(memory_space=pltpu.VMEM)] * 3,
        out_specs=pl.BlockSpec(memory_space=pltpu.VMEM),
        scratch_shapes=[
            vm((4, 2, 128, 128), F32),
            vm((2, 4, 4, 4, 8, 128), F32),
            vm((8, 128), jnp.int32),
            vm((16, 8, 128), jnp.int32),
            pltpu.SMEM((16, 8, 128), jnp.int32),
            vm((128, 128), jnp.int32),
            pltpu.SMEM((128, 128), jnp.int32),
            vm((4, 4, 4, 2, 32, 128), F32),
            vm((2, 4, 2, 2, 8, 4, 8, 128), F32),
            vm((1025, 4, 8, 128), F32),
            vm((16, 8, 128), jnp.int32),
            vm((2, 512, 256), BF16),
            vm((2, 256, 256), BF16),
            vm((2, 2, 4, 256, 128), F32),
            vm((2, 2, 2, 128, 128), F32),
            vm((2, 4, 256, 128), F32),
            vm((2, 4, 2, 64, 128), F32),
            vm((2, 4, 2, 64, 128), F32),
            dma((2, 15)), dma((2, 15)), dma((5,)), dma((5,)), dma((4,)), dma((4,)), dma((2, 4)), dma((2, 4)), dma((4,)), dma((4,)),
            dma((4, 2)), dma((4, 2)), dma((5,)), dma((5,)), dma((2, 2)), dma((2, 2)), dma((2, 2, 2)), dma((2, 2, 2)),
            dma((2, 4)), dma((2, 4)), dma((4,)),
        ],
        compiler_params=pltpu.CompilerParams(collective_id=0, has_side_effects=True),
        name="square",
    )(p_vals, p_cols, out_cols)


def solution(mesh):
    placed = (P("row", "col", None, None), P("row", None), P("row", None))
    return jax.shard_map(
        on_device,
        mesh=mesh,
        in_specs=placed,
        out_specs=P("row", "col", None, None),
        check_vma=False,
    )
```

```python
import jax
import jax.numpy as jnp
from jax import lax
from jax.experimental import pallas as pl
from jax.experimental.pallas import tpu as pltpu
from jax.sharding import PartitionSpec as P

MESH = pl.DeviceIdType.MESH
F32 = jnp.float32
BF16 = jnp.bfloat16
NX, NY, NZ = 4, 4, 8
WAY = (0, 1, 0, 1)


def up(v, d, n):
    return lax.rem(v + (d + n), n)


def kernel(p_ref, pc_ref, oc_ref, out_ref, pt, tb, mown, mbuf, sm, ix, ixs, ag, bg, rot, pvs, mt, aw, ct, r1, r2, fo, fi,
           tbs, tbr, ms, mr, ays, ayr, axs, axr, afs, afr, zs, zr, cs, cr, us, ur, vs, vr, fs, fr, loc):
    row = lax.axis_index("row")
    col = lax.axis_index("col")
    z, yh, q = lax.div(row, 4), lax.rem(lax.div(row, 2), 2), lax.rem(row, 2)
    yl, x = lax.div(col, 4), lax.rem(col, 4)
    y = 2 * yh + yl

    def dev(x_, y_, z_, q_):
        return (z_ * 4 + lax.div(y_, 2) * 2 + q_, lax.rem(y_, 2) * 4 + x_)

    def rcopy(src, dst, s, r, to):
        return pltpu.make_async_remote_copy(
            src_ref=src, dst_ref=dst, send_sem=s, recv_sem=r, device_id=to, device_id_type=MESH
        )

    started = []

    def go(c):
        c.start()
        started.append(c)
        return c

    plane = [(dx, dy) for dy in range(NY) for dx in range(NX) if (dx, dy) != (0, 0)]
    lower, upper, mate = dev(x, y, up(z, -1, NZ), q), dev(x, y, up(z, 1, NZ), q), dev(x, y, z, 1 - q)
    xp, xm = up(x, 1, NX), up(x, -1, NX)
    right, left = dev(xp, y, z, q), dev(xm, y, z, q)
    yp, ym, yf = up(y, 1, NY), up(y, -1, NY), up(y, 2, NY)
    above, below = dev(x, yp, z, q), dev(x, ym, z, q)

    barrier = pltpu.get_barrier_semaphore()
    for to in [dev(up(x, -dx, NX), up(y, -dy, NY), z, q) for dx, dy in plane] + [lower, upper, mate]:
        pl.semaphore_signal(barrier, inc=1, device_id=to, device_id_type=MESH)

    mown[...] = jnp.zeros((8, 128), jnp.int32)
    mown[0:4, 0:16] = pc_ref[...]
    mown[4:8, 0:16] = oc_ref[...]
    lane = lax.div(lax.broadcasted_iota(jnp.int32, (128, 128), 1), 32)
    for e in range(2):
        for l in range(4):
            pt[l, e] = p_ref[l, e].T
        for yy in range(NY):
            packed = None
            for l in range(4):
                t = pt[l, e]
                if l != yy:
                    t = pltpu.roll(t, (32 * (l - yy)) % 128, 1)
                packed = t if packed is None else jnp.where(lane == l, t, packed)
            for xx in range(NX):
                tb[e, yy, xx] = packed[32 * xx:32 * xx + 32].reshape(4, 8, 128)
    rot[1024] = jnp.zeros((4, 8, 128), F32)
    for m in range(2):
        aw[m, 128:256, 128:256] = jnp.zeros((128, 128), BF16)

    pl.semaphore_wait(barrier, len(plane) + 3)

    my = go(rcopy(mown, mbuf.at[q * 8 + 2 + yh], ms.at[0], mr.at[0], dev(x, yf, z, q)))
    own = [pltpu.make_async_copy(mown, mbuf.at[q * 8 + 2 + yh], loc.at[0])]
    own += [pltpu.make_async_copy(tb.at[e, y, x], bg.at[q, 1, yh, e, col], loc.at[1 + e]) for e in range(2)]
    own += [pltpu.make_async_copy(pt.at[:, :, pl.ds(32 * y, 32)], ag.at[x, y], loc.at[3])]
    for c in own:
        c.start()

    def pieces(e):
        out = []
        for n, (dx, dy) in enumerate(plane):
            xx, yy = up(x, dx, NX), up(y, dy, NY)
            out.append(go(rcopy(tb.at[e, yy, xx], bg.at[q, 1, yh, e, col], tbs.at[e, n], tbr.at[e, n], dev(xx, yy, z, q))))
        return out

    b0 = pieces(0)
    rows_y = pt.at[:, :, pl.ds(32 * y, 32)]

    def beside(src, ys):
        return [rcopy(src, ag.at[x, ys], axs.at[n, ys], axr.at[n, ys], (right, left)[n]) for n in range(2)]

    for c in beside(rows_y, y):
        c.start()
    for dy in (1, 3, 2):
        if dy == 2:
            b1 = pieces(1)
        yy = up(y, dy, NY)
        go(rcopy(pt.at[:, :, pl.ds(32 * yy, 32)], ag.at[x, y], ays.at[dy], ayr.at[y], dev(x, yy, z, q)))

    for c in own:
        c.wait()
    my.wait_recv()
    m2 = go(rcopy(mbuf.at[pl.ds(q * 8 + 2, 2)], mbuf.at[pl.ds(q * 8 + 4, 2)], ms.at[1], mr.at[1], lower))
    m0 = go(rcopy(mbuf.at[q * 8 + 3], mbuf.at[q * 8 + 1], ms.at[2], mr.at[2], upper))
    m2.wait_recv()
    m3 = go(rcopy(mbuf.at[pl.ds(q * 8 + 4, 2)], mbuf.at[pl.ds(q * 8 + 6, 2)], ms.at[3], mr.at[3], lower))

    def level1(e):
        a = go(rcopy(bg.at[q, 1, :, e], bg.at[q, 2, :, e], zs.at[0, e], zr.at[0, e], lower))
        b = go(rcopy(bg.at[q, 1, 1, e], bg.at[q, 0, 1, e], zs.at[1, e], zr.at[1, e], upper))
        return a, b

    for c in b0:
        c.wait_recv()
    za0, zb0 = level1(0)
    m0.wait_recv()
    m3.wait_recv()
    mm = go(rcopy(mbuf.at[pl.ds(q * 8 + 1, 7)], mbuf.at[pl.ds(q * 8 + 1, 7)], ms.at[4], mr.at[4], mate))
    mm.wait_recv()
    mc = pltpu.make_async_copy(mbuf, sm, loc.at[0])
    mc.start()
    mc.wait()

    direct = [beside(ag.at[x, ys], ys) for ys in range(NY)]

    def arrived(dy):
        ys = up(y, dy, NY)
        rcopy(rows_y, ag.at[x, ys], ays.at[0], ayr.at[ys], right).wait_recv()
        for c in beside(ag.at[x, ys], ys):
            c.start()

    arrived(1)
    arrived(3)
    for c in b1:
        c.wait_recv()
    za1, zb1 = level1(1)
    c1 = go(rcopy(bg.at[q, 1], bg.at[q, 1], cs.at[0], cr.at[0], mate))

    arrived(2)

    def pick(i, carry):
        h, l, s4 = lax.div(i, 16), lax.rem(lax.div(i, 4), 4), lax.rem(i, 4)
        mine = q * 8 + 2 + h
        outs = mbuf[mine, pl.ds(4 + l, 1)]
        for j in range(4):
            s = 4 * s4 + j
            k = sm[mine, l, s]
            g = lax.div(k, 4)
            kk = lax.rem(k, 4)
            w = lax.rem(4 * z + 2 * h + q + lax.div(s, 2) - g + 64, 32) < 3
            lev = jnp.where(w, lax.rem(lax.div(g, 4) - z + 9, 8), 1)
            slot = lax.rem(g, 2) * 8 + lev * 2 + lax.rem(lax.div(g, 2), 2)
            base = (lax.rem(j + 4 - kk, 4) * 16 + slot) * 16
            v = jnp.full((1, 128), 1024, jnp.int32)
            for p in range(16):
                v = jnp.where(outs == sm[slot, kk, 2 * (p % 8) + p // 8], base + p, v)
            ix[pl.ds(i * 4 + j, 1)] = jnp.where(w, v, 1024)
        return carry

    lax.fori_loop(0, 32, pick, 0)
    ic = pltpu.make_async_copy(ix, ixs, loc.at[0])
    ic.start()

    def onward(ys):
        n = WAY[ys]
        direct[ys][n].wait_recv()
        ref = ag.at[(xm, xp)[n], ys]
        return go(rcopy(ref, ref, afs.at[ys], afr.at[ys], (right, left)[n]))

    lane8 = lax.div(lax.broadcasted_iota(jnp.int32, (8, 128), 1), 32)
    sel = [lane8 == j for j in range(3)]

    def spread(v):
        r = jnp.where(sel[2], v[2], v[3])
        r = jnp.where(sel[1], v[1], r)
        return jnp.where(sel[0], v[0], r)

    def expand(qs, lev, h):
        slot = qs * 8 + lev * 2 + h
        for p in range(16):
            pvs[p] = spread([sm[slot, l, 2 * (p % 8) + p // 8] for l in range(4)])

        def step(i, carry):
            acc = [jnp.zeros((4, 8, 128), F32)] * 2
            v = [pvs[2 * i + n] for n in range(2)]
            for p in range(16):
                b = bg[qs, lev, h, p // 8, p % 8]
                w = pvs[p]
                for n in range(2):
                    acc[n] = acc[n] + jnp.where((w == v[n])[None], b, 0.0)
            for n in range(2):
                t = acc[n].reshape(32, 128)
                for k in range(4):
                    u = t if k == 0 else pltpu.roll(t, 32 * k, 1)
                    rot[(k * 16 + slot) * 16 + 2 * i + n] = u.reshape(4, 8, 128)
            return carry
        lax.fori_loop(0, 8, step, 0)

    def both(qs, lev):
        def step(h, carry):
            expand(qs, lev, h)
            return carry
        lax.fori_loop(0, 2, step, 0)

    def level2(e, za):
        za.wait_recv()
        a = go(rcopy(bg.at[q, 2, 0, e], bg.at[q, 3, 0, e], zs.at[2, e], zr.at[2, e], lower))
        return a

    zc0 = level2(0, za0)
    both(q, 1)
    c1.wait_recv()
    both(1 - q, 1)

    zc1 = level2(1, za1)
    zd = [rcopy(bg.at[0, 2, 1, e], bg.at[0, 3, 1, e], zs.at[3, e], zr.at[3, e], lower) for e in range(2)]

    @pl.when(q == 0)
    def _():
        for c in zd:
            c.start()

    c2 = go(rcopy(bg.at[q, 2], bg.at[q, 2], cs.at[1], cr.at[1], mate))
    far = [onward(0), onward(1)]
    zb0.wait_recv()
    zb1.wait_recv()
    c0 = rcopy(bg.at[1, 0, 1], bg.at[1, 0, 1], cs.at[4], cr.at[4], mate)

    @pl.when(q == 1)
    def _():
        c0.start()

    both(q, 2)
    far += [onward(2), onward(3)]
    c2.wait_recv()
    both(1 - q, 2)

    @pl.when(q == 0)
    def _():
        c0.wait_recv()

    expand(1, 0, 1)

    @pl.when(q == 0)
    def _():
        expand(0, 0, 1)

    def product(h, l, s4, m, first):
        for o in range(16):
            a = spread([rot[ixs[(h * 4 + l) * 16 + 4 * s4 + j, o]] for j in range(4)]).reshape(32, 128)
            hi = a.astype(BF16)
            mt[m, 32 * o:32 * o + 32, 0:128] = hi
            mt[m, 32 * o:32 * o + 32, 128:256] = (a - hi.astype(F32)).astype(BF16)
        a = ag[pl.ds(2 * lax.rem(s4, 2), 2), 2 * h + lax.div(s4, 2), l].reshape(128, 128)
        hi = a.astype(BF16)
        aw[m, 0:128, 0:128] = hi
        aw[m, 0:128, 128:256] = (a - hi.astype(F32)).astype(BF16)
        aw[m, 128:256, 0:128] = hi
        r = jnp.dot(mt[m], aw[m], preferred_element_type=F32)
        r = r[:, :128] + r[:, 128:]
        for half in range(2):
            part = r[256 * half:256 * half + 256]
            ct[h, half, l] = part if first else ct[h, half, l] + part

    def early(h):
        for ys in (2 * h, 2 * h + 1):
            direct[ys][1 - WAY[ys]].wait_recv()
            far[ys].wait_recv()
        for s4 in range(2):
            def step(i, carry, s4=s4):
                for m in range(2):
                    product(h, 2 * i + m, s4, m, s4 == 0)
                return carry
            lax.fori_loop(0, 2, step, 0)

    ic.wait()
    early(0)
    zc0.wait_recv()
    zc1.wait_recv()
    c3a = go(rcopy(bg.at[q, 3, 0], bg.at[q, 3, 0], cs.at[2], cr.at[2], mate))
    c3b = rcopy(bg.at[0, 3, 1], bg.at[0, 3, 1], cs.at[3], cr.at[3], mate)
    expand(q, 3, 0)
    @pl.when(q == 0)
    def _():
        for c in zd:
            c.wait_recv()
        c3b.start()

    early(1)

    c3a.wait_recv()
    expand(1 - q, 3, 0)

    @pl.when(q == 1)
    def _():
        c3b.wait_recv()
        expand(0, 3, 1)

    def piece(y_, lp, part):
        return ct.at[lax.div(y_, 2), lax.rem(y_, 2), pl.ds(2 * lp, 2), pl.ds(128 * part, 128)]

    def rest(h, lp):
        def step(i, carry):
            for m in range(2):
                product(h, 2 * lp + m, 2 + i, m, False)
            return carry
        lax.fori_loop(0, 2, step, 0)

    def hop1(d, lp):
        return go(rcopy(piece(yf, lp, d), r1.at[d, lp], us.at[d, lp], ur.at[d, lp], (above, below)[d]))

    def hop2(d, part, lp):
        return go(rcopy(piece((yp, ym)[d], lp, part), r2.at[d, pl.ds(2 * lp, 2), pl.ds(128 * part, 128)],
                        vs.at[d, part, lp], vr.at[d, part, lp], (above, below)[d]))

    u, v = {}, {}
    for lp in range(2):
        rest(1 - yh, lp)
        for d in range(2):
            u[d, lp] = hop1(d, lp)
    for lp in range(2):
        rest(yh, lp)
        for d in range(2):
            v[d, 1 - d, lp] = hop2(d, 1 - d, lp)
    for lp in range(2):
        for d in range(2):
            u[d, lp].wait_recv()
            a = piece((yp, ym)[d], lp, d)
            a[...] = a[...] + r1[d, lp]
            v[d, d, lp] = hop2(d, d, lp)

    fsend = {}
    for lp in range(2):
        for d in range(2):
            for part in range(2):
                v[d, part, lp].wait_recv()
        for k in range(2):
            l = 2 * lp + k
            t = ct[yh, yl, l] + r2[0, l] + r2[1, l]
            for xx in range(NX):
                fo[lp, xx, k] = t[64 * xx:64 * xx + 64]
        for dx in range(1, NX):
            xx = up(x, dx, NX)
            fsend[lp, dx] = go(rcopy(fo.at[lp, xx], fi.at[lp, x], fs.at[lp, dx], fr.at[lp, dx], dev(xx, y, z, q)))
        fsend[lp, 0] = pltpu.make_async_copy(fo.at[lp, x], fi.at[lp, x], loc.at[lp])
        fsend[lp, 0].start()
    for lp in range(2):
        fsend[lp, 0].wait()
        for dx in range(1, NX):
            fsend[lp, dx].wait_recv()
        for k in range(2):
            for e in range(2):
                t = jnp.concatenate([fi[lp, xx, k, 32 * e:32 * e + 32] for xx in range(NX)], axis=0)
                out_ref[2 * lp + k, e] = t.T

    for c in started + [c for k in direct for c in k]:
        c.wait_send()

    @pl.when(q == 0)
    def _():
        for c in zd:
            c.wait_send()
        c3b.wait_send()

    @pl.when(q == 1)
    def _():
        c0.wait_send()


def on_device(p_vals, p_cols, out_cols):
    dma = pltpu.SemaphoreType.DMA
    vm = pltpu.VMEM
    return pl.pallas_call(
        kernel,
        out_shape=jax.ShapeDtypeStruct((4, 2, 128, 128), F32),
        in_specs=[pl.BlockSpec(memory_space=pltpu.VMEM)] * 3,
        out_specs=pl.BlockSpec(memory_space=pltpu.VMEM),
        scratch_shapes=[
            vm((4, 2, 128, 128), F32),
            vm((2, 4, 4, 4, 8, 128), F32),
            vm((8, 128), jnp.int32),
            vm((16, 8, 128), jnp.int32),
            pltpu.SMEM((16, 8, 128), jnp.int32),
            vm((128, 128), jnp.int32),
            pltpu.SMEM((128, 128), jnp.int32),
            vm((4, 4, 4, 2, 32, 128), F32),
            vm((2, 4, 2, 2, 8, 4, 8, 128), F32),
            vm((1025, 4, 8, 128), F32),
            vm((16, 8, 128), jnp.int32),
            vm((2, 512, 256), BF16),
            vm((2, 256, 256), BF16),
            vm((2, 2, 4, 256, 128), F32),
            vm((2, 2, 2, 128, 128), F32),
            vm((2, 4, 256, 128), F32),
            vm((2, 4, 2, 64, 128), F32),
            vm((2, 4, 2, 64, 128), F32),
            dma((2, 15)), dma((2, 15)), dma((5,)), dma((5,)), dma((4,)), dma((4,)), dma((2, 4)), dma((2, 4)), dma((4,)), dma((4,)),
            dma((4, 2)), dma((4, 2)), dma((5,)), dma((5,)), dma((2, 2)), dma((2, 2)), dma((2, 2, 2)), dma((2, 2, 2)),
            dma((2, 4)), dma((2, 4)), dma((4,)),
        ],
        compiler_params=pltpu.CompilerParams(collective_id=0, has_side_effects=True),
        name="square",
    )(p_vals, p_cols, out_cols)


def solution(mesh):
    placed = (P("row", "col", None, None), P("row", None), P("row", None))
    return jax.shard_map(
        on_device,
        mesh=mesh,
        in_specs=placed,
        out_specs=P("row", "col", None, None),
        check_vma=False,
    )
```
